256 devices in a mesh: pair: 32 (over x, y, core), slab: 8 (over z).
Axes of the slice: x: 4, y: 4, z: 8, core: 2. Of those that a mesh axis runs over, the one named last changes fastest.
Arguments:
- amplitudes: bfloat16 [6144, 9216], P('pair', 'slab'), may hold values from -6 to 6
- integrals: bfloat16 [9216, 9216], P('slab', 'pair'), may hold values from -0.125 to 0.125
- pair_index: int32 [6144, 2], P('pair'), may hold values from 0 to 159, as said below
- eps_occ: float32 [160], replicated, may hold values from -2 to -0.5
- eps_vir: float32 [96], replicated, may hold values from 0.5 to 3
Outputs:
- update: float32 [6144, 9216], P('pair', 'slab')
The draws below stay inside these ranges and needn't reach their ends.
Inputs may be any that keep to these rules, and one draw needn't show every extreme that they name: `pair_index`: each row holds i < j; pairs may repeat; pair 0 is (0, 159).
All inputs are finite; a program needn't handle non-finite values.
Results may differ from the reference program's by a relative error of at most 0.0003.
Values may be sent and summed in bfloat16 or wider, within the bound.
A program may use at most 128 MiB of HBM per device.

```python
import jax
import jax.numpy as jnp

NOCC = 160
NA = 96
PAIRS = 6144
VV = 9216


def draw_pair_index(key, part):
    key_one, key_two = jax.random.split(jax.random.fold_in(key, 7))
    first = jax.random.randint(key_one, (PAIRS,), 0, NOCC - 1)
    second = jax.random.randint(key_two, (PAIRS,), first + 1, NOCC)
    first = first.at[0].set(0)
    second = second.at[0].set(NOCC - 1)
    return jnp.stack([first, second], axis=1).astype(jnp.int32)


def spiked(values, key, source, target, shards_of, factor):
    def block_of(position):
        return (jnp.arange(values.shape[position]) // (values.shape[position] // shards_of)).reshape((-1,) + (1,) * (values.ndim - 1 - position))

    one_side = jax.random.permutation(key, shards_of)[block_of(target)]
    other_side = (block_of(target) + shards_of // 2) % shards_of
    return jnp.where((block_of(source) == one_side) | (block_of(source) == other_side), factor * values, values)


def block_levels(key, shape, pieces, low, largest):
    factor_of = 1.0
    for position, parts in pieces:
        draws = jax.random.uniform(jax.random.fold_in(jax.random.fold_in(key, 6), position), (parts,), jnp.float32, low / len(pieces), largest / len(pieces))
        factor_of = factor_of * jnp.repeat(jnp.exp(draws), shape[position] // parts).reshape((-1,) + (1,) * (len(shape) - 1 - position))
    return factor_of


def scatter_about(stream_key, extent, spread, reach, cuts=(), dtype=jnp.bfloat16):
    values = jax.random.normal(stream_key, extent, jnp.float32) * spread
    if len(cuts) > 0:
        values = block_levels(stream_key, extent, cuts, -0.22, 0.18) * values
    return jnp.clip(values, min=-reach, max=reach).astype(dtype)


def gaussian_with(own_key, shape, scale, reach, pieces, heavy, held_as=jnp.bfloat16):
    values = scale * jax.random.normal(own_key, shape, jnp.float32)
    if pieces:
        values = values * block_levels(own_key, shape, pieces, -0.22, 0.18)
    return jnp.clip(spiked(values, jax.random.fold_in(own_key, 3), *heavy), -reach, reach).astype(held_as)


def setup_inputs(seed: int = 0) -> dict:
    seeds = jax.random.split(jax.random.key(seed), 6)
    return {
        "amplitudes": scatter_about(seeds[0], (PAIRS, VV), 1.0, 6.0, ((0, 32), (1, 8))),
        "integrals": gaussian_with(seeds[1], (VV, VV), VV ** -0.5, 0.125, ((0, 8), (1, 32)), (0, 1, 32, 2.75)),
        "pair_index": draw_pair_index(jax.random.fold_in(seeds[5], 71), 0),
        "eps_occ": jnp.clip(jax.random.uniform(seeds[3], (NOCC,), jnp.float32, -2.0, -0.5), -2.0, -0.5),
        "eps_vir": jnp.clip(jax.random.uniform(seeds[4], (NA,), jnp.float32, 0.5, 3.0), 0.5, 3.0),
    }


def reference(amplitudes, integrals, pair_index, eps_occ, eps_vir):
    ladder = jnp.dot(amplitudes, integrals, preferred_element_type=jnp.float32)
    ladder_cube = ladder.reshape(PAIRS, NA, NA)
    antisym = (ladder_cube - jnp.swapaxes(ladder_cube, 1, 2)).reshape(PAIRS, NA * NA)
    e_pair = eps_occ[pair_index[:, 0]] + eps_occ[pair_index[:, 1]]
    e_virt = (eps_vir[:, None] + eps_vir[None, :]).reshape(NA * NA)
    return antisym / (e_pair[:, None] - e_virt[None, :])
```

```python
import functools

import jax
import jax.numpy as jnp
import numpy as np
from jax import lax
from jax.experimental import pallas as pl
from jax.experimental.pallas import tpu as pltpu
from jax.sharding import PartitionSpec as P

MESH = pl.DeviceIdType.MESH
G = 12
ROWS = 40
HALF = 72
QMAX = 32767.0


def selection_tables():
    sel = np.zeros((3, 2, HALF, 4 * ROWS), np.float32)
    for kind in range(3):
        for i in range(6):
            for v in range(G):
                u, vv = i, v
                if kind == 1:
                    u = i + 6
                if kind == 2 and v < i:
                    u, vv = i + 6, v + 6
                sel[kind, 0, i * G + v, ROWS * (u // 3) + G * (u % 3) + vv] = 1
                sel[kind, 1, i * G + v, ROWS * (vv // 3) + G * (vv % 3) + u] = 1
    return sel


def output_tables():
    table = np.zeros((8, 4, G * 8 * G), np.int32)
    for w in range(8):
        for a in range(G):
            for o in range(8):
                for b in range(G):
                    col = (a * 8 + o) * G + b
                    if o > w:
                        u, v, s, h = a, b, 1, a // 6
                    elif o < w:
                        u, v, s, h = b, a, -1, b // 6
                    else:
                        lo, hi, s, h = min(a, b), max(a, b), (0 if a == b else 1 if a < b else -1), 0
                        if lo >= 6:
                            u, v, s = hi - 6, lo - 6, -s
                        else:
                            u, v = lo, hi
                    table[w, :, col] = (o * 2 + h) * HALF + (u % 6) * G + v, w * G + a, o * G + b, s
    return table


def row_order():
    order = np.zeros((8 * ROWS, 3 * 8 * G), np.float32)
    for o in range(8):
        for a in range(3):
            for b in range(G):
                order[o * ROWS + a * G + b, (a * 8 + o) * G + b] = 1
    return order


def xor3(a, b):
    out = 0
    for bit in (1, 2, 4):
        out = out + bit * lax.rem(lax.div(a, bit) + lax.div(b, bit), 2)
    return out


def quantize(val, q_ref, s_ref):
    n, r, width = val.shape
    cube = val.reshape(n * r // 8, 8, width)
    top = jnp.maximum(jnp.max(jnp.abs(cube), axis=0) * (1.01 / QMAX), 1e-36).astype(jnp.bfloat16)
    q = (cube * (1.0 / top.astype(jnp.float32)) + 32768.5).astype(jnp.int32) - 32768
    q_ref[...] = q.reshape(n, r, width).astype(jnp.int16)
    s_ref[...] = top


def dequantize(q, s):
    n, r, width = q.shape
    cube = q.astype(jnp.int32).astype(jnp.float32).reshape(n * r // 8, 8, width)
    return (cube * s.astype(jnp.float32)).reshape(n, r, width)


def column(row):
    n = row.shape[1]
    same = lax.broadcasted_iota(jnp.int32, (n, n), 0) == lax.broadcasted_iota(jnp.int32, (n, n), 1)
    return jnp.sum(jnp.where(same, row, 0.0), axis=1, keepdims=True)


def looked_up(ids, table):
    hit = lax.broadcasted_iota(jnp.int32, (table.shape[0], ids.shape[1]), 0) == ids
    return jnp.sum(jnp.where(hit, table, 0.0), axis=0, keepdims=True)


def kernel(sel_ref, order_ref, table_ref, a_ref, vt_ref, pairs_ref, occ_ref, vir_ref, out_ref,
           a_all, v_ref, v_buf, v1, v2, cs, rq, rs, sq, ss, fq, fs, gq, gs, w_ref, o_ref, ep_ref, ev_ref,
           vx_s, vx_r, vy_s, vy_r, vf_s, vf_r, ax_s, ax_r, af_s, af_r, ap_s, ap_r, own_s,
           rq_s, rq_r, rs_s, rs_r, fq_s, fq_r, fs_s, fs_r):
    pair, z = lax.axis_index("pair"), lax.axis_index("slab")
    x, y, c = lax.div(pair, 8), lax.rem(lax.div(pair, 2), 4), lax.rem(pair, 2)

    def kid(xx, cc):
        return xx + 4 * cc

    kappa = kid(x, c)
    w_mine = lax.div(pair, 4)

    def dev(xx, yy, cc, zz):
        return ((xx * 4 + yy) * 2 + cc, zz)

    def step(i, d, n):
        return lax.rem(i + d + n, n)

    def remote(src, dst, ssem, rsem, to):
        return pltpu.make_async_remote_copy(
            src_ref=src, dst_ref=dst, send_sem=ssem, recv_sem=rsem, device_id=to, device_id_type=MESH
        )

    barrier = pltpu.get_barrier_semaphore()

    def greet(to):
        pl.semaphore_signal(barrier, inc=1, device_id=to, device_id_type=MESH)

    for dx in range(4):
        for dc in range(2):
            if dx or dc:
                greet(dev(step(x, dx, 4), y, step(c, dc, 2), z))
    for d in (1, -1):
        greet(dev(x, step(y, d, 4), c, z))
        greet(dev(x, y, c, step(z, d, 8)))
    ordered = jnp.dot(order_ref[...], vt_ref[...], preferred_element_type=jnp.float32).astype(jnp.bfloat16)
    v_ref[...] = ordered.reshape(v_ref.shape)
    pl.semaphore_wait(barrier, 11)

    slot_y = lax.rem(y, 2) * 2
    copies = []
    for dx in (1, 3, 2, 0):
        for dc in (0, 1):
            xx, cc = step(x, dx, 4), step(c, dc, 2)
            k = kid(xx, cc)
            src = v_ref.at[xor3(w_mine, k)]
            dst = v_buf.at[w_mine, slot_y + c]
            if dx or dc:
                cp = remote(src, dst, vx_s.at[dx * 2 + dc], vx_r.at[kappa], dev(xx, y, cc, z))
            else:
                cp = pltpu.make_async_copy(src, dst, own_s.at[0])
            cp.start()
            copies.append((dx or dc, cp))
    for d, di in ((1, 0), (-1, 1)):
        for h in range(2):
            part = pl.ds(96 * h, 96)
            remote(a_ref.at[part], a_all.at[x, c, part], ax_s.at[di, h], ax_r.at[di, h], dev(step(x, d, 4), y, c, z)).start()
    other = dev(x, y, 1 - c, z)
    remote(a_ref, a_all.at[x, c], ap_s.at[0], ap_r.at[0], other).start()
    own_a = pltpu.make_async_copy(a_ref, a_all.at[x, c], own_s.at[1])
    own_a.start()

    def v_slot(yy, xx, cc):
        return v_buf.at[2 * xx + lax.div(yy, 2), lax.rem(yy, 2) * 2 + cc]

    def to_y(d):
        return dev(x, step(y, d, 4), c, z)

    for dx in (0, 1, 3, 2):
        for dc in range(2):
            xx, cc = step(x, dx, 4), step(c, dc, 2)
            blk = v_slot(y, xx, cc)
            if dx or dc:
                remote(blk, blk, vx_s.at[0], vx_r.at[kid(xx, cc)], other).wait_recv()
            else:
                copies[-2][1].wait()
            for d, di in ((1, 0), (-1, 1)):
                u = dx * 2 + cc
                remote(blk, blk, vy_s.at[di, u], vy_r.at[di, u], to_y(d)).start()

    for d, di in ((1, 0), (-1, 1)):
        blk = a_all.at[step(x, -d, 4), c, pl.ds(96 * di, 96)]
        remote(blk, blk, ax_s.at[di, di], ax_r.at[di, di], other).wait_recv()
        remote(blk, blk, af_s.at[di], af_r.at[di], dev(step(x, d, 4), y, c, z)).start()

    table = table_ref[z]
    sign = table[3:4].astype(jnp.float32)

    @pl.loop(0, 9)
    def _(i):
        rows = lax.broadcasted_iota(jnp.int32, (128, 8 * G * G), 0) + i * 128
        hit = rows == table[0:1]
        w_ref[pl.ds(pl.multiple_of(i * 128, 128), 128), :] = jnp.where(hit, sign, 0.0).astype(jnp.bfloat16)

    vir, occ = column(vir_ref[...]), column(occ_ref[...])
    ev_ref[...] = looked_up(table[1:2], vir) + looked_up(table[2:3], vir)
    ep_ref[...] = column(looked_up(pairs_ref[0:1], occ) + looked_up(pairs_ref[1:2], occ))

    for dx in (0, 1, 3, 2):
        for d, di in ((1, 0), (-1, 1)):
            u = dx * 2 + di
            blk = v_slot(step(y, -d, 4), step(x, dx, 4), di)
            remote(blk, blk, vy_s.at[di, u], vy_r.at[di, u], other).wait_recv()
            remote(blk, blk, vf_s.at[u], vf_r.at[u], to_y(d)).start()

    for n, d, di in ((1, 1, 0), (2, -1, 1)):
        blk = a_all.at[step(x, -d, 4), c]
        part = a_all.at[step(x, -d, 4), c, pl.ds(96 * (1 - di), 96)]
        remote(part, part, ax_s.at[di, 1 - di], ax_r.at[di, 1 - di], other).wait_recv()
        remote(blk, blk, ap_s.at[n], ap_r.at[n], other).start()
    far = a_all.at[step(x, 2, 4), c]
    for di in range(2):
        part = a_all.at[step(x, 2, 4), c, pl.ds(96 * di, 96)]
        remote(part, part, af_s.at[di], af_r.at[di], other).wait_recv()
    remote(far, far, ap_s.at[3], ap_r.at[3], other).start()

    for d, di in ((1, 0), (-1, 1)):
        for dx in (0, 1, 3, 2):
            u = dx * 2 + 1 - di
            blk = v_slot(step(y, -d, 4), step(x, dx, 4), 1 - di)
            remote(blk, blk, vy_s.at[di, u], vy_r.at[di, u], other).wait_recv()
    for dx in (0, 1, 3, 2):
        for di in range(2):
            u = dx * 2 + di
            blk = v_slot(step(y, 2, 4), step(x, dx, 4), di)
            remote(blk, blk, vf_s.at[u], vf_r.at[u], other).wait_recv()

    targets = (4, 3, -3, 2, -2, 1, -1, 0)

    def select(j):
        t = step(z, targets[j], 8)
        o = xor3(t, kappa)
        lo, hi = jnp.minimum(t, o), jnp.maximum(t, o)
        kind = jnp.where(kappa == 0, 2, jnp.where(t == lo, 0, 1))
        rows = pl.ds(j * HALF, HALF)
        v1[rows, :] = jnp.dot(
            sel_ref[kind, 0], v_buf[lo].reshape(4 * ROWS, -1), preferred_element_type=jnp.float32
        ).astype(jnp.bfloat16)
        v2[rows, :] = jnp.dot(
            sel_ref[kind, 1], v_buf[hi].reshape(4 * ROWS, -1), preferred_element_type=jnp.float32
        ).astype(jnp.bfloat16)

    nt = (((1,), (1,)), ((), ()))

    def products(first, last):
        rows = pl.ds(first * HALF, (last - first) * HALF)

        @pl.loop(0, 4)
        def _(i):
            rows_a = a_all[i].reshape(2 * a_all.shape[2], -1)
            cs[i, rows] = lax.dot_general(
                v1[rows, :], rows_a, nt, preferred_element_type=jnp.float32
            ) - lax.dot_general(v2[rows, :], rows_a, nt, preferred_element_type=jnp.float32)

    for j in range(3):
        select(j)
    own_a.wait()
    for n, dx in ((0, 0), (1, -1), (2, 1), (3, 2)):
        blk = a_all.at[step(x, dx, 4), 1 - c]
        remote(blk, blk, ap_s.at[n], ap_r.at[n], other).wait_recv()

    products(0, 3)

    def chunk(t, h):
        j = targets.index(4 if t == -4 else t)
        return cs[pl.ds(2 * h, 2), pl.ds(j * HALF, HALF), :]

    streams = [(1, 0, 3), (-1, 0, 4), (1, 1, 4), (-1, 1, 3)]

    def hop(i, s, d):
        to = dev(x, y, c, step(z, d, 8))
        return (
            remote(sq.at[i, s], rq.at[i, s], rq_s.at[i, s], rq_r.at[i, s], to),
            remote(ss.at[i, s], rs.at[i, s], rs_s.at[i, s], rs_r.at[i, s], to),
        )

    for s in range(4):
        for i, (d, h, length) in enumerate(streams):
            if s >= length:
                continue
            val = chunk(d * (length - s), h)
            if s:
                for cp in hop(i, s - 1, d):
                    cp.wait_recv()
                val = val + dequantize(rq[i, s - 1], rs[i, s - 1])
            quantize(val, sq.at[i, s], ss.at[i, s])
            for cp in hop(i, s, d):
                cp.start()
        if s == 0:
            for j in range(3, 8):
                select(j)
            products(3, 8)

    gq[2 * z + 1] = jnp.zeros(gq.shape[1:], gq.dtype)
    gs[2 * z + 1] = jnp.zeros(gs.shape[1:], gs.dtype)
    for h in range(2):
        val = chunk(0, h)
        for i, (d, hh, length) in enumerate(streams):
            if hh == h:
                for cp in hop(i, length - 1, d):
                    cp.wait_recv()
                val = val + dequantize(rq[i, length - 1], rs[i, length - 1])
        for i in range(2):
            quantize(val[i : i + 1], fq.at[pl.ds(2 * h + i, 1)], fs.at[2 * h + i])

    o = xor3(z, kappa)
    end = jnp.where(z > o, 1, 0)

    def deliver(dx, dc, mirror):
        xx, cc = step(x, dx, 4), step(c, dc, 2)
        lanes = pl.ds(pl.multiple_of(128 * cc, 128), 256)
        slot = 2 * (z if mirror else o) + end
        n, m = (dx * 2 + dc), int(mirror)
        to = dev(xx, y, cc, o if mirror else z)
        if not (dx or dc or mirror):
            return (
                pltpu.make_async_copy(fq.at[xx, :, lanes], gq.at[slot], own_s.at[2]),
                pltpu.make_async_copy(fs.at[xx, :, lanes], gs.at[slot], own_s.at[3]),
            )
        return (
            remote(fq.at[xx, :, lanes], gq.at[slot], fq_s.at[m, n], fq_r.at[m, kappa], to),
            remote(fs.at[xx, :, lanes], gs.at[slot], fs_s.at[m, n], fs_r.at[m, kappa], to),
        )

    order = [(dx, dc) for dx in (2, 1, 3, 0) for dc in (0, 1)]

    @pl.when(kappa > 0)
    def _():
        for dx, dc in order:
            for cp in deliver(dx, dc, True):
                cp.start()

    for dx, dc in order:
        for cp in deliver(dx, dc, False):
            cp.start()

    def arrived(m, k):
        remote(fq.at[0, :, pl.ds(0, 256)], gq.at[0], fq_s.at[0, 0], fq_r.at[m, k], other).wait_recv()
        remote(fs.at[0, :, pl.ds(0, 256)], gs.at[0], fs_s.at[0, 0], fs_r.at[m, k], other).wait_recv()

    tn = (((0,), (0,)), ((), ()))
    for n, (dx, dc) in enumerate(((0, 0), (0, 1), (1, 0), (1, 1), (3, 0), (3, 1), (2, 0), (2, 1))):
        k = kid(step(x, dx, 4), step(c, dc, 2))
        if dx or dc:
            arrived(0, k)
        else:
            for cp in deliver(0, 0, False):
                cp.wait()

        @pl.when(k > 0)
        def _():
            arrived(1, k)

        o = xor3(z, k)
        full = jnp.concatenate(
            [dequantize(gq[pl.ds(2 * o + i, 1)], gs[2 * o + i])[0] for i in range(2)], axis=0
        )
        top = full.astype(jnp.bfloat16)
        low = (full - top.astype(jnp.float32)).astype(jnp.bfloat16)
        w_rows = w_ref[pl.ds(pl.multiple_of(o * 2 * HALF, 16), 2 * HALF), :]
        part = lax.dot_general(top, w_rows, tn, preferred_element_type=jnp.float32) + lax.dot_general(
            low, w_rows, tn, preferred_element_type=jnp.float32
        )
        o_ref[...] = part if n == 0 else o_ref[...] + part
    out_ref[...] = o_ref[pl.ds(pl.multiple_of(64 * c, 8), out_ref.shape[0]), :] / (ep_ref[...] - ev_ref[...])

    for dx in range(4):
        for dc in range(2):
            n = dx * 2 + dc
            if n:
                remote(v_ref.at[0], v_buf.at[0, 0], vx_s.at[n], vx_r.at[0], other).wait_send()
            for di in range(2):
                remote(v_ref.at[0], v_buf.at[0, 0], vy_s.at[di, n], vx_r.at[0], other).wait_send()
            remote(v_ref.at[0], v_buf.at[0, 0], vf_s.at[n], vx_r.at[0], other).wait_send()
    half_a = a_ref.at[pl.ds(0, 96)]
    for di in range(2):
        for h in range(2):
            remote(half_a, half_a, ax_s.at[di, h], ax_r.at[di, h], other).wait_send()
        remote(half_a, half_a, af_s.at[di], af_r.at[di], other).wait_send()
    for n in range(4):
        remote(a_ref, a_ref, ap_s.at[n], ap_r.at[n], other).wait_send()
    for i, (d, h, length) in enumerate(streams):
        for s in range(length):
            for cp in hop(i, s, d):
                cp.wait_send()
    for dx, dc in order:
        if dx or dc:
            for cp in deliver(dx, dc, False):
                cp.wait_send()

    @pl.when(kappa > 0)
    def _():
        for dx, dc in order:
            for cp in deliver(dx, dc, True):
                cp.wait_send()


def on_device(amplitudes, integrals, pair_index, eps_occ, eps_vir):
    rows, depth = amplitudes.shape
    f32, bf16, i16 = jnp.float32, jnp.bfloat16, jnp.int16
    dma = pltpu.SemaphoreType.DMA
    return pl.pallas_call(
        kernel,
        out_shape=jax.ShapeDtypeStruct((rows, 8 * G * G), f32),
        in_specs=[pl.BlockSpec(memory_space=pltpu.VMEM)] * 8,
        out_specs=pl.BlockSpec(memory_space=pltpu.VMEM),
        scratch_shapes=[
            pltpu.VMEM((4, 2, rows, depth), bf16),
            pltpu.VMEM((8, ROWS, depth), bf16),
            pltpu.VMEM((8, 4, ROWS, depth), bf16),
            pltpu.VMEM((8 * HALF, depth), bf16),
            pltpu.VMEM((8 * HALF, depth), bf16),
            pltpu.VMEM((4, 8 * HALF, 2 * rows), f32),
            pltpu.VMEM((4, 4, 2, HALF, 2 * rows), i16),
            pltpu.VMEM((4, 4, 8, 2 * rows), bf16),
            pltpu.VMEM((4, 4, 2, HALF, 2 * rows), i16),
            pltpu.VMEM((4, 4, 8, 2 * rows), bf16),
            pltpu.VMEM((4, HALF, 2 * rows), i16),
            pltpu.VMEM((4, 8, 2 * rows), bf16),
            pltpu.VMEM((16, HALF, 256), i16),
            pltpu.VMEM((16, 8, 256), bf16),
            pltpu.VMEM((16 * HALF, 8 * G * G), bf16),
            pltpu.VMEM((256, 8 * G * G), f32),
            pltpu.VMEM((rows, 1), f32),
            pltpu.VMEM((1, 8 * G * G), f32),
            dma((8,)), dma((8,)), dma((2, 8)), dma((2, 8)), dma((8,)), dma((8,)),
            dma((2, 2)), dma((2, 2)), dma((2,)), dma((2,)), dma((4,)), dma((4,)), dma((4,)),
            dma((4, 4)), dma((4, 4)), dma((4, 4)), dma((4, 4)),
            dma((2, 8)), dma((2, 8)), dma((2, 8)), dma((2, 8)),
        ],
        compiler_params=pltpu.CompilerParams(
            collective_id=0, has_side_effects=True, vmem_limit_bytes=60 * 1024 * 1024
        ),
    )(
        jnp.asarray(selection_tables(), bf16),
        jnp.asarray(row_order(), bf16),
        jnp.asarray(output_tables()),
        amplitudes,
        integrals.T,
        pair_index.T,
        eps_occ.reshape(1, -1),
        eps_vir.reshape(1, -1),
    )


def solution(mesh):
    in_specs = (P("pair", "slab"), P("slab", "pair"), P("pair", None), P(), P())
    return jax.shard_map(on_device, mesh=mesh, in_specs=in_specs, out_specs=P("pair", "slab"), check_vma=False)
```

```python
import functools

import jax
import jax.numpy as jnp
import numpy as np
from jax import lax
from jax.experimental import pallas as pl
from jax.experimental.pallas import tpu as pltpu
from jax.sharding import PartitionSpec as P

MESH = pl.DeviceIdType.MESH
G = 12
ROWS = 40
HALF = 72
QMAX = 32767.0


def selection_tables():
    sel = np.zeros((3, 2, HALF, 4 * ROWS), np.float32)
    for kind in range(3):
        for i in range(6):
            for v in range(G):
                u, vv = i, v
                if kind == 1:
                    u = i + 6
                if kind == 2 and v < i:
                    u, vv = i + 6, v + 6
                sel[kind, 0, i * G + v, ROWS * (u // 3) + G * (u % 3) + vv] = 1
                sel[kind, 1, i * G + v, ROWS * (vv // 3) + G * (vv % 3) + u] = 1
    return sel


def output_tables():
    table = np.zeros((8, 4, G * 8 * G), np.int32)
    for w in range(8):
        for a in range(G):
            for o in range(8):
                for b in range(G):
                    col = (a * 8 + o) * G + b
                    if o > w:
                        u, v, s, h = a, b, 1, a // 6
                    elif o < w:
                        u, v, s, h = b, a, -1, b // 6
                    else:
                        lo, hi, s, h = min(a, b), max(a, b), (0 if a == b else 1 if a < b else -1), 0
                        if lo >= 6:
                            u, v, s = hi - 6, lo - 6, -s
                        else:
                            u, v = lo, hi
                    table[w, :, col] = (o * 2 + h) * HALF + (u % 6) * G + v, w * G + a, o * G + b, s
    return table


def row_order():
    order = np.zeros((8 * ROWS, 3 * 8 * G), np.float32)
    for o in range(8):
        for a in range(3):
            for b in range(G):
                order[o * ROWS + a * G + b, (a * 8 + o) * G + b] = 1
    return order


def xor3(a, b):
    out = 0
    for bit in (1, 2, 4):
        out = out + bit * lax.rem(lax.div(a, bit) + lax.div(b, bit), 2)
    return out


def quantize(val, q_ref, s_ref):
    r, width = val.shape
    cube = val.reshape(r // 8, 8, width)
    top = jnp.max(jnp.abs(cube), axis=0)
    top = functools.reduce(jnp.maximum, [top[:, 128 * i : 128 * (i + 1)] for i in range(width // 128)])
    top = jnp.maximum(top * (1.01 / QMAX), 1e-36).astype(jnp.bfloat16)
    inv = 1.0 / top.astype(jnp.float32)
    q = (cube * jnp.concatenate([inv] * (width // 128), axis=1) + 32768.5).astype(jnp.int32) - 32768
    q_ref[...] = q.reshape(r, width).astype(jnp.int16)
    s_ref[...] = top


def dequantize(q, s):
    r, width = q.shape
    cube = q.astype(jnp.int32).astype(jnp.float32).reshape(r // 8, 8, width)
    return (cube * jnp.concatenate([s.astype(jnp.float32)] * (width // 128), axis=1)).reshape(r, width)


def column(row):
    n = row.shape[1]
    same = lax.broadcasted_iota(jnp.int32, (n, n), 0) == lax.broadcasted_iota(jnp.int32, (n, n), 1)
    return jnp.sum(jnp.where(same, row, 0.0), axis=1, keepdims=True)


def looked_up(ids, table):
    hit = lax.broadcasted_iota(jnp.int32, (table.shape[0], ids.shape[1]), 0) == ids
    return jnp.sum(jnp.where(hit, table, 0.0), axis=0, keepdims=True)


def kernel(sel_hbm, order_hbm, table_hbm, a_hbm, vt_hbm, pairs_hbm, occ_hbm, vir_hbm, out_hbm,
           sel_ref, order_ref, table_ref, vt_ref, pairs_ref, occ_ref, vir_ref, in_s, out_s, out_ref,
           a_all, v_ref, v_buf, v1, v2, cs, rq, rs, sq, ss, fq, fs, gq, gs, w_ref, o_ref, ep_ref, ev_ref,
           vx_s, vx_r, vy_s, vy_r, vf_s, vf_r, ax_s, ax_r, af_s, af_r, ap_s, ap_r, own_s,
           rq_s, rq_r, rs_s, rs_r, fq_s, fq_r, fs_s, fs_r):
    pair, z = lax.axis_index("pair"), lax.axis_index("slab")
    x, y, c = lax.div(pair, 8), lax.rem(lax.div(pair, 2), 4), lax.rem(pair, 2)

    def kid(xx, cc):
        return xx + 4 * cc

    kappa = kid(x, c)
    w_mine = lax.div(pair, 4)

    def dev(xx, yy, cc, zz):
        return ((xx * 4 + yy) * 2 + cc, zz)

    def step(i, d, n):
        return lax.rem(i + d + n, n)

    def remote(src, dst, ssem, rsem, to):
        return pltpu.make_async_remote_copy(
            src_ref=src, dst_ref=dst, send_sem=ssem, recv_sem=rsem, device_id=to, device_id_type=MESH
        )

    a_ref = a_all.at[x, c]
    inputs = [
        pltpu.make_async_copy(src, dst, in_s.at[i])
        for i, (src, dst) in enumerate(
            (
                (order_hbm, order_ref), (vt_hbm, vt_ref), (a_hbm, a_ref), (table_hbm, table_ref), (sel_hbm, sel_ref),
                (pairs_hbm, pairs_ref), (occ_hbm, occ_ref), (vir_hbm, vir_ref),
            )
        )
    ]
    for cp in inputs:
        cp.start()

    barrier = pltpu.get_barrier_semaphore()

    def greet(to):
        pl.semaphore_signal(barrier, inc=1, device_id=to, device_id_type=MESH)

    for dx in range(4):
        for dc in range(2):
            if dx or dc:
                greet(dev(step(x, dx, 4), y, step(c, dc, 2), z))
    for d in (1, -1):
        greet(dev(x, step(y, d, 4), c, z))
        greet(dev(x, y, c, step(z, d, 8)))
    inputs[0].wait()
    inputs[1].wait()
    ordered = jnp.dot(order_ref[...], vt_ref[...], preferred_element_type=jnp.float32).astype(jnp.bfloat16)
    v_ref[...] = ordered.reshape(v_ref.shape)
    pl.semaphore_wait(barrier, 11)

    slot_y = lax.rem(y, 2) * 2
    copies = []
    for dx in (1, 3, 2, 0):
        for dc in (0, 1):
            xx, cc = step(x, dx, 4), step(c, dc, 2)
            k = kid(xx, cc)
            src = v_ref.at[xor3(w_mine, k)]
            dst = v_buf.at[w_mine, slot_y + c]
            if dx or dc:
                cp = remote(src, dst, vx_s.at[dx * 2 + dc], vx_r.at[kappa], dev(xx, y, cc, z))
            else:
                cp = pltpu.make_async_copy(src, dst, own_s.at[0])
            cp.start()
            copies.append((dx or dc, cp))
    inputs[2].wait()
    for d, di in ((1, 0), (-1, 1)):
        for h in range(2):
            part = a_all.at[x, c, pl.ds(96 * h, 96)]
            remote(part, part, ax_s.at[di, h], ax_r.at[di, h], dev(step(x, d, 4), y, c, z)).start()
    other = dev(x, y, 1 - c, z)
    remote(a_ref, a_ref, ap_s.at[0], ap_r.at[0], other).start()

    def v_slot(yy, xx, cc):
        return v_buf.at[2 * xx + lax.div(yy, 2), lax.rem(yy, 2) * 2 + cc]

    def to_y(d):
        return dev(x, step(y, d, 4), c, z)

    for dx in (0, 1, 3, 2):
        for dc in range(2):
            xx, cc = step(x, dx, 4), step(c, dc, 2)
            blk = v_slot(y, xx, cc)
            if dx or dc:
                remote(blk, blk, vx_s.at[0], vx_r.at[kid(xx, cc)], other).wait_recv()
            else:
                copies[-2][1].wait()
            for d, di in ((1, 0), (-1, 1)):
                u = dx * 2 + cc
                remote(blk, blk, vy_s.at[di, u], vy_r.at[di, u], to_y(d)).start()

    for d, di in ((1, 0), (-1, 1)):
        blk = a_all.at[step(x, -d, 4), c, pl.ds(96 * di, 96)]
        remote(blk, blk, ax_s.at[di, di], ax_r.at[di, di], other).wait_recv()
        remote(blk, blk, af_s.at[di], af_r.at[di], dev(step(x, d, 4), y, c, z)).start()

    for cp in inputs[3:]:
        cp.wait()
    table = table_ref[z]
    sign = table[3:4].astype(jnp.float32)

    @pl.loop(0, 9)
    def _(i):
        rows = lax.broadcasted_iota(jnp.int32, (128, 8 * G * G), 0) + i * 128
        hit = rows == table[0:1]
        w_ref[pl.ds(pl.multiple_of(i * 128, 128), 128), :] = jnp.where(hit, sign, 0.0).astype(jnp.bfloat16)

    vir, occ = column(vir_ref[...]), column(occ_ref[...])
    ev_ref[...] = looked_up(table[1:2], vir) + looked_up(table[2:3], vir)
    ep_ref[...] = column(looked_up(pairs_ref[0:1], occ) + looked_up(pairs_ref[1:2], occ))

    for dx in (0, 1, 3, 2):
        for d, di in ((1, 0), (-1, 1)):
            u = dx * 2 + di
            blk = v_slot(step(y, -d, 4), step(x, dx, 4), di)
            remote(blk, blk, vy_s.at[di, u], vy_r.at[di, u], other).wait_recv()
            remote(blk, blk, vf_s.at[u], vf_r.at[u], to_y(d)).start()

    for n, d, di in ((1, 1, 0), (2, -1, 1)):
        blk = a_all.at[step(x, -d, 4), c]
        part = a_all.at[step(x, -d, 4), c, pl.ds(96 * (1 - di), 96)]
        remote(part, part, ax_s.at[di, 1 - di], ax_r.at[di, 1 - di], other).wait_recv()
        remote(blk, blk, ap_s.at[n], ap_r.at[n], other).start()
    far = a_all.at[step(x, 2, 4), c]
    for di in range(2):
        part = a_all.at[step(x, 2, 4), c, pl.ds(96 * di, 96)]
        remote(part, part, af_s.at[di], af_r.at[di], other).wait_recv()
    remote(far, far, ap_s.at[3], ap_r.at[3], other).start()

    for d, di in ((1, 0), (-1, 1)):
        for dx in (0, 1, 3, 2):
            u = dx * 2 + 1 - di
            blk = v_slot(step(y, -d, 4), step(x, dx, 4), 1 - di)
            remote(blk, blk, vy_s.at[di, u], vy_r.at[di, u], other).wait_recv()
    for dx in (0, 1, 3, 2):
        for di in range(2):
            u = dx * 2 + di
            blk = v_slot(step(y, 2, 4), step(x, dx, 4), di)
            remote(blk, blk, vf_s.at[u], vf_r.at[u], other).wait_recv()

    targets = (4, 3, -3, 2, -2, 1, -1, 0)

    def select(j):
        t = step(z, targets[j], 8)
        o = xor3(t, kappa)
        lo, hi = jnp.minimum(t, o), jnp.maximum(t, o)
        kind = jnp.where(kappa == 0, 2, jnp.where(t == lo, 0, 1))
        rows = pl.ds(j * HALF, HALF)
        v1[rows, :] = jnp.dot(
            sel_ref[kind, 0], v_buf[lo].reshape(4 * ROWS, -1), preferred_element_type=jnp.float32
        ).astype(jnp.bfloat16)
        v2[rows, :] = jnp.dot(
            sel_ref[kind, 1], v_buf[hi].reshape(4 * ROWS, -1), preferred_element_type=jnp.float32
        ).astype(jnp.bfloat16)

    nt = (((1,), (1,)), ((), ()))

    rel = (0, 1, 3, 2)

    def products(groups, first, last):
        rows = pl.ds(first * HALF, (last - first) * HALF)

        @pl.loop(groups[0], groups[1])
        def _(g):
            rows_a = a_all[step(x, jnp.where(g < 2, g, 5 - g), 4)].reshape(2 * a_all.shape[2], -1)
            cs[g, rows] = lax.dot_general(
                v1[rows, :], rows_a, nt, preferred_element_type=jnp.float32
            ) - lax.dot_general(v2[rows, :], rows_a, nt, preferred_element_type=jnp.float32)

    for j in range(3):
        select(j)

    def other_core(n, dx):
        blk = a_all.at[step(x, dx, 4), 1 - c]
        remote(blk, blk, ap_s.at[n], ap_r.at[n], other).wait_recv()

    other_core(0, 0)
    other_core(2, 1)
    products((0, 2), 0, 3)

    def chunk(t, g):
        j = targets.index(4 if t == -4 else t)
        return cs[g, pl.ds(j * HALF, HALF), :]

    def streams(g):
        return ((1, 0, 3 + g % 2), (-1, 1, 4 - g % 2))

    def hop(g, i, s, d):
        to = dev(x, y, c, step(z, d, 8))
        return (
            remote(sq.at[g, i, s], rq.at[g, i, s], rq_s.at[g, i, s], rq_r.at[g, i, s], to),
            remote(ss.at[g, i, s], rs.at[g, i, s], rs_s.at[g, i, s], rs_r.at[g, i, s], to),
        )

    def incoming(g, i, s, d):
        for cp in hop(g, i, s, d):
            cp.wait_recv()
        return dequantize(rq[g, i, s], rs[g, i, s])

    def advance(groups, s):
        for g in groups:
            for d, i, length in streams(g):
                if s < length:
                    val = chunk(d * (length - s), g)
                    if s:
                        val = val + incoming(g, i, s - 1, d)
                    quantize(val, sq.at[g, i, s], ss.at[g, i, s])
                    for cp in hop(g, i, s, d):
                        cp.start()

    o_mine = xor3(z, kappa)
    end = jnp.where(z > o_mine, 1, 0)

    def deliver(g, dc, mirror):
        xx, cc = step(x, rel[g], 4), step(c, dc, 2)
        lanes = pl.ds(pl.multiple_of(128 * cc, 128), 256)
        slot = 2 * (z if mirror else o_mine) + end
        n, m = g * 2 + dc, int(mirror)
        to = dev(xx, y, cc, o_mine if mirror else z)
        if not (g or dc or mirror):
            return (
                pltpu.make_async_copy(fq.at[g, :, lanes], gq.at[slot], own_s.at[2]),
                pltpu.make_async_copy(fs.at[g], gs.at[slot], own_s.at[3]),
            )
        return (
            remote(fq.at[g, :, lanes], gq.at[slot], fq_s.at[m, n], fq_r.at[m, kappa], to),
            remote(fs.at[g], gs.at[slot], fs_s.at[m, n], fs_r.at[m, kappa], to),
        )

    def finish(groups):
        for g in groups:
            val = chunk(0, g)
            for d, i, length in streams(g):
                val = val + incoming(g, i, length - 1, d)
            quantize(val, fq.at[g], fs.at[g])

            @pl.when(kappa > 0)
            def _():
                for dc in (0, 1):
                    for cp in deliver(g, dc, True):
                        cp.start()

            for dc in (0, 1):
                for cp in deliver(g, dc, False):
                    cp.start()

    advance((0, 1), 0)
    for j in (3, 4):
        select(j)
    products((0, 2), 3, 5)
    advance((0, 1), 1)
    for j in (5, 6, 7):
        select(j)
    products((0, 2), 5, 8)
    other_core(1, -1)
    other_core(3, 2)
    products((2, 4), 0, 3)
    advance((0, 1), 2)
    advance((2, 3), 0)
    products((2, 4), 3, 8)
    advance((0, 1), 3)
    advance((2, 3), 1)
    gq[2 * z + 1] = jnp.zeros(gq.shape[1:], gq.dtype)
    gs[2 * z + 1] = jnp.zeros(gs.shape[1:], gs.dtype)
    finish((0, 1))
    advance((2, 3), 2)
    advance((2, 3), 3)
    finish((2, 3))

    def arrived(m, k):
        remote(fq.at[0, :, pl.ds(0, 256)], gq.at[0], fq_s.at[0, 0], fq_r.at[m, k], other).wait_recv()
        remote(fs.at[0], gs.at[0], fs_s.at[0, 0], fs_r.at[m, k], other).wait_recv()

    tn = (((0,), (0,)), ((), ()))
    for n, (dx, dc) in enumerate(((0, 0), (0, 1), (3, 0), (3, 1), (1, 0), (1, 1), (2, 0), (2, 1))):
        k = kid(step(x, dx, 4), step(c, dc, 2))
        if dx or dc:
            arrived(0, k)
        else:
            for cp in deliver(0, 0, False):
                cp.wait()

        @pl.when(k > 0)
        def _():
            arrived(1, k)

        o = xor3(z, k)
        full = jnp.concatenate(
            [dequantize(gq[2 * o + i], gs[2 * o + i]) for i in range(2)], axis=0
        )
        top = full.astype(jnp.bfloat16)
        low = (full - top.astype(jnp.float32)).astype(jnp.bfloat16)
        w_rows = w_ref[pl.ds(pl.multiple_of(o * 2 * HALF, 16), 2 * HALF), :]
        part = lax.dot_general(top, w_rows, tn, preferred_element_type=jnp.float32) + lax.dot_general(
            low, w_rows, tn, preferred_element_type=jnp.float32
        )
        o_ref[...] = part if n == 0 else o_ref[...] + part
    leaving = []
    for i in range(3):
        rows = pl.ds(64 * i, 64)
        out_ref[rows, :] = o_ref[pl.ds(pl.multiple_of(64 * (c + i), 8), 64), :] / (ep_ref[rows, :] - ev_ref[...])
        leaving.append(pltpu.make_async_copy(out_ref.at[rows], out_hbm.at[rows], out_s.at[i]))
        leaving[-1].start()

    for dx in range(4):
        for dc in range(2):
            n = dx * 2 + dc
            if n:
                remote(v_ref.at[0], v_buf.at[0, 0], vx_s.at[n], vx_r.at[0], other).wait_send()
            for di in range(2):
                remote(v_ref.at[0], v_buf.at[0, 0], vy_s.at[di, n], vx_r.at[0], other).wait_send()
            remote(v_ref.at[0], v_buf.at[0, 0], vf_s.at[n], vx_r.at[0], other).wait_send()
    half_a = a_all.at[0, 0, pl.ds(0, 96)]
    for di in range(2):
        for h in range(2):
            remote(half_a, half_a, ax_s.at[di, h], ax_r.at[di, h], other).wait_send()
        remote(half_a, half_a, af_s.at[di], af_r.at[di], other).wait_send()
    for n in range(4):
        remote(a_ref, a_ref, ap_s.at[n], ap_r.at[n], other).wait_send()
    for g in range(4):
        for d, i, length in streams(g):
            for s in range(length):
                for cp in hop(g, i, s, d):
                    cp.wait_send()
        for dc in (0, 1):
            if g or dc:
                for cp in deliver(g, dc, False):
                    cp.wait_send()

    @pl.when(kappa > 0)
    def _():
        for g in range(4):
            for dc in (0, 1):
                for cp in deliver(g, dc, True):
                    cp.wait_send()

    for cp in leaving:
        cp.wait()


def on_device(amplitudes, integrals, pair_index, eps_occ, eps_vir):
    rows, depth = amplitudes.shape
    f32, bf16, i16 = jnp.float32, jnp.bfloat16, jnp.int16
    dma = pltpu.SemaphoreType.DMA
    sel, order = jnp.asarray(selection_tables(), bf16), jnp.asarray(row_order(), bf16)
    table = jnp.asarray(output_tables())
    vt, pairs, occ, vir = integrals.T, pair_index.T, eps_occ.reshape(1, -1), eps_vir.reshape(1, -1)
    return pl.pallas_call(
        kernel,
        out_shape=jax.ShapeDtypeStruct((rows, 8 * G * G), f32),
        in_specs=[pl.BlockSpec(memory_space=pl.ANY)] * 8,
        out_specs=pl.BlockSpec(memory_space=pl.ANY),
        scratch_shapes=[
            *[pltpu.VMEM(a.shape, a.dtype) for a in (sel, order, table, vt, pairs, occ, vir)],
            dma((8,)),
            dma((3,)),
            pltpu.VMEM((rows, 8 * G * G), f32),
            pltpu.VMEM((4, 2, rows, depth), bf16),
            pltpu.VMEM((8, ROWS, depth), bf16),
            pltpu.VMEM((8, 4, ROWS, depth), bf16),
            pltpu.VMEM((8 * HALF, depth), bf16),
            pltpu.VMEM((8 * HALF, depth), bf16),
            pltpu.VMEM((4, 8 * HALF, 2 * rows), f32),
            pltpu.VMEM((4, 2, 4, HALF, 2 * rows), i16),
            pltpu.VMEM((4, 2, 4, 8, 128), bf16),
            pltpu.VMEM((4, 2, 4, HALF, 2 * rows), i16),
            pltpu.VMEM((4, 2, 4, 8, 128), bf16),
            pltpu.VMEM((4, HALF, 2 * rows), i16),
            pltpu.VMEM((4, 8, 128), bf16),
            pltpu.VMEM((16, HALF, 256), i16),
            pltpu.VMEM((16, 8, 128), bf16),
            pltpu.VMEM((16 * HALF, 8 * G * G), bf16),
            pltpu.VMEM((256, 8 * G * G), f32),
            pltpu.VMEM((rows, 1), f32),
            pltpu.VMEM((1, 8 * G * G), f32),
            dma((8,)), dma((8,)), dma((2, 8)), dma((2, 8)), dma((8,)), dma((8,)),
            dma((2, 2)), dma((2, 2)), dma((2,)), dma((2,)), dma((4,)), dma((4,)), dma((4,)),
            dma((4, 2, 4)), dma((4, 2, 4)), dma((4, 2, 4)), dma((4, 2, 4)),
            dma((2, 8)), dma((2, 8)), dma((2, 8)), dma((2, 8)),
        ],
        compiler_params=pltpu.CompilerParams(
            collective_id=0, has_side_effects=True, vmem_limit_bytes=60 * 1024 * 1024
        ),
    )(sel, order, table, amplitudes, vt, pairs, occ, vir)


def solution(mesh):
    in_specs = (P("pair", "slab"), P("slab", "pair"), P("pair", None), P(), P())
    return jax.shard_map(on_device, mesh=mesh, in_specs=in_specs, out_specs=P("pair", "slab"), check_vma=False)
```

```python
import functools

import jax
import jax.numpy as jnp
import numpy as np
from jax import lax
from jax.experimental import pallas as pl
from jax.experimental.pallas import tpu as pltpu
from jax.sharding import PartitionSpec as P

MESH = pl.DeviceIdType.MESH
G = 12
BLOCK = (24, 16)
OWN = (48, 24)
QMAX = 32767.0


def chunk_of(u, v):
    return 0 if (u + v) % 3 else 1


def block_row(u, v):
    q = chunk_of(u, v)
    rank = sum(chunk_of(u, i) == q for i in range(v))
    return BLOCK[q] * (u // 3) + (8, 4)[q] * (u % 3) + rank


def own_row(i, v):
    q = chunk_of(i, v)
    return (8, 4)[q] * i + sum(chunk_of(i, j) == q for j in range(v))


def selection_tables():
    sel = [np.zeros((3, 2, OWN[q], 4 * BLOCK[q]), np.float32) for q in range(2)]
    for kind in range(3):
        for i in range(6):
            for v in range(G):
                u, vv = i, v
                if kind == 1:
                    u = i + 6
                if kind == 2 and v < i:
                    u, vv = i + 6, v + 6
                q = chunk_of(i, v)
                sel[q][kind, 0, own_row(i, v), block_row(u, vv)] = 1
                sel[q][kind, 1, own_row(i, v), block_row(vv, u)] = 1
    return sel


def output_tables():
    table = np.zeros((8, 4, G * 8 * G), np.int32)
    for w in range(8):
        for a in range(G):
            for o in range(8):
                for b in range(G):
                    col = (a * 8 + o) * G + b
                    if o > w:
                        u, v, s, h = a, b, 1, a // 6
                    elif o < w:
                        u, v, s, h = b, a, -1, b // 6
                    else:
                        lo, hi, s, h = min(a, b), max(a, b), (0 if a == b else 1 if a < b else -1), 0
                        if lo >= 6:
                            u, v, s = hi - 6, lo - 6, -s
                        else:
                            u, v = lo, hi
                    q = chunk_of(u, v)
                    row = 16 * OWN[0] * q + (o * 2 + h) * OWN[q] + own_row(u % 6, v)
                    table[w, :, col] = row, w * G + a, o * G + b, s
    return table


def row_order():
    order = np.zeros((8 * sum(BLOCK), 3 * 8 * G), np.float32)
    for o in range(8):
        for a in range(3):
            for b in range(G):
                q = chunk_of(a, b)
                order[8 * BLOCK[0] * q + o * BLOCK[q] + block_row(a, b), (a * 8 + o) * G + b] = 1
    return order


def xor3(a, b):
    out = 0
    for bit in (1, 2, 4):
        out = out + bit * lax.rem(lax.div(a, bit) + lax.div(b, bit), 2)
    return out


def quantize(val, q_ref, s_ref):
    r, width = val.shape
    cube = val.reshape(r // 8, 8, width)
    top = jnp.max(jnp.abs(cube), axis=0)
    top = functools.reduce(jnp.maximum, [top[:, 128 * i : 128 * (i + 1)] for i in range(width // 128)])
    top = jnp.maximum(top * (1.01 / QMAX), 1e-36).astype(jnp.bfloat16)
    inv = 1.0 / top.astype(jnp.float32)
    q = (cube * jnp.concatenate([inv] * (width // 128), axis=1) + 32768.5).astype(jnp.int32) - 32768
    q_ref[...] = q.reshape(r, width).astype(jnp.int16)
    s_ref[...] = top


def dequantize(q, s):
    r, width = q.shape
    cube = q.astype(jnp.int32).astype(jnp.float32).reshape(r // 8, 8, width)
    return (cube * jnp.concatenate([s.astype(jnp.float32)] * (width // 128), axis=1)).reshape(r, width)


def column(row):
    n = row.shape[1]
    same = lax.broadcasted_iota(jnp.int32, (n, n), 0) == lax.broadcasted_iota(jnp.int32, (n, n), 1)
    return jnp.sum(jnp.where(same, row, 0.0), axis=1, keepdims=True)


def looked_up(ids, table):
    hit = lax.broadcasted_iota(jnp.int32, (table.shape[0], ids.shape[1]), 0) == ids
    return jnp.sum(jnp.where(hit, table, 0.0), axis=0, keepdims=True)


def kernel(sel0_hbm, sel1_hbm, order_hbm, table_hbm, a_hbm, vt_hbm, pairs_hbm, occ_hbm, vir_hbm, out_hbm,
           sel0, sel1, order_ref, table_ref, vt_ref, pairs_ref, occ_ref, vir_ref, in_s, out_s, out_ref,
           a_all, w_ref, o_ref, ep_ref, ev_ref,
           vl0, vl1, vb0, vb1, va0, va1, vc0, vc1, cs0, cs1, rq0, rq1, sq0, sq1, fq0, fq1, gq0, gq1,
           rs, ss, fs, gs,
           vx_s, vx_r, vy_s, vy_r, vf_s, vf_r, ax_s, ax_r, af_s, af_r, ap_s, ap_r, own_s,
           rq_s, rq_r, rs_s, rs_r, fq_s, fq_r, fs_s, fs_r):
    sel, v_local, v_buf, v_one, v_two, cs = (sel0, sel1), (vl0, vl1), (vb0, vb1), (va0, va1), (vc0, vc1), (cs0, cs1)
    rq, sq, fq, gq = (rq0, rq1), (sq0, sq1), (fq0, fq1), (gq0, gq1)
    pair, z = lax.axis_index("pair"), lax.axis_index("slab")
    x, y, c = lax.div(pair, 8), lax.rem(lax.div(pair, 2), 4), lax.rem(pair, 2)

    def kid(xx, cc):
        return xx + 4 * cc

    kappa = kid(x, c)
    w_mine = lax.div(pair, 4)

    def dev(xx, yy, cc, zz):
        return ((xx * 4 + yy) * 2 + cc, zz)

    def step(i, d, n):
        return lax.rem(i + d + n, n)

    def remote(src, dst, ssem, rsem, to):
        return pltpu.make_async_remote_copy(
            src_ref=src, dst_ref=dst, send_sem=ssem, recv_sem=rsem, device_id=to, device_id_type=MESH
        )

    other = dev(x, y, 1 - c, z)
    a_ref = a_all.at[x, c]
    inputs = [
        pltpu.make_async_copy(src, dst, in_s.at[i])
        for i, (src, dst) in enumerate(
            (
                (order_hbm, order_ref), (vt_hbm, vt_ref), (a_hbm, a_ref), (table_hbm, table_ref), (sel0_hbm, sel0),
                (sel1_hbm, sel1), (pairs_hbm, pairs_ref), (occ_hbm, occ_ref), (vir_hbm, vir_ref),
            )
        )
    ]
    for cp in inputs:
        cp.start()

    barrier = pltpu.get_barrier_semaphore()

    def greet(to):
        pl.semaphore_signal(barrier, inc=1, device_id=to, device_id_type=MESH)

    for dx in range(4):
        for dc in range(2):
            if dx or dc:
                greet(dev(step(x, dx, 4), y, step(c, dc, 2), z))
    for d in (1, -1):
        greet(dev(x, step(y, d, 4), c, z))
        greet(dev(x, y, c, step(z, d, 8)))
    inputs[0].wait()
    inputs[1].wait()
    ordered = jnp.dot(order_ref[...], vt_ref[...], preferred_element_type=jnp.float32).astype(jnp.bfloat16)
    v_local[0][...] = ordered[: 8 * BLOCK[0]].reshape(v_local[0].shape)
    v_local[1][...] = ordered[8 * BLOCK[0] :].reshape(v_local[1].shape)
    pl.semaphore_wait(barrier, 11)

    slot_y = lax.rem(y, 2) * 2
    ring = (0, 1, 3, 2)

    def to_class(q, dx, dc):
        xx, cc = step(x, dx, 4), step(c, dc, 2)
        src = v_local[q].at[xor3(w_mine, kid(xx, cc))]
        dst = v_buf[q].at[w_mine, slot_y + c]
        if dx or dc:
            return remote(src, dst, vx_s.at[q, dx * 2 + dc], vx_r.at[q, kappa], dev(xx, y, cc, z))
        return pltpu.make_async_copy(src, dst, own_s.at[0, q])

    for q in range(2):
        for dx in (1, 3, 2, 0):
            for dc in (0, 1):
                to_class(q, dx, dc).start()
    inputs[2].wait()
    for h in range(2):
        for d, di in ((1, 0), (-1, 1)):
            hh = h if di == 0 else 1 - h
            part = a_all.at[x, c, pl.ds(96 * hh, 96)]
            remote(part, part, ax_s.at[di, hh], ax_r.at[di, hh], dev(step(x, d, 4), y, c, z)).start()
    remote(a_ref, a_ref, ap_s.at[0], ap_r.at[0], other).start()

    def v_slot(q, yy, xx, cc):
        return v_buf[q].at[2 * xx + lax.div(yy, 2), lax.rem(yy, 2) * 2 + cc]

    def to_y(d):
        return dev(x, step(y, d, 4), c, z)

    def spread(q):
        for dx in ring:
            for dc in range(2):
                xx, cc = step(x, dx, 4), step(c, dc, 2)
                blk = v_slot(q, y, xx, cc)
                if dx or dc:
                    remote(blk, blk, vx_s.at[q, 0], vx_r.at[q, kid(xx, cc)], other).wait_recv()
                else:
                    to_class(q, 0, 0).wait()
                for d, di in ((1, 0), (-1, 1)):
                    u = dx * 2 + cc
                    remote(blk, blk, vy_s.at[q, di, u], vy_r.at[q, di, u], to_y(d)).start()

    def pass_on(q):
        for dx in ring:
            for d, di in ((1, 0), (-1, 1)):
                u = dx * 2 + di
                blk = v_slot(q, step(y, -d, 4), step(x, dx, 4), di)
                remote(blk, blk, vy_s.at[q, di, u], vy_r.at[q, di, u], other).wait_recv()
                remote(blk, blk, vf_s.at[q, u], vf_r.at[q, u], to_y(d)).start()

    def gathered(q):
        for d, di in ((1, 0), (-1, 1)):
            for dx in ring:
                u = dx * 2 + 1 - di
                blk = v_slot(q, step(y, -d, 4), step(x, dx, 4), 1 - di)
                remote(blk, blk, vy_s.at[q, di, u], vy_r.at[q, di, u], other).wait_recv()
        for dx in ring:
            for di in range(2):
                u = dx * 2 + di
                blk = v_slot(q, step(y, 2, 4), step(x, dx, 4), di)
                remote(blk, blk, vf_s.at[q, u], vf_r.at[q, u], other).wait_recv()

    def pass_on_a():
        for d, di in ((1, 0), (-1, 1)):
            blk = a_all.at[step(x, -d, 4), c, pl.ds(96 * di, 96)]
            remote(blk, blk, ax_s.at[di, di], ax_r.at[di, di], other).wait_recv()
            remote(blk, blk, af_s.at[di], af_r.at[di], dev(step(x, d, 4), y, c, z)).start()

    def share_near():
        for n, d, di in ((1, 1, 0), (2, -1, 1)):
            blk = a_all.at[step(x, -d, 4), c]
            part = a_all.at[step(x, -d, 4), c, pl.ds(96 * (1 - di), 96)]
            remote(part, part, ax_s.at[di, 1 - di], ax_r.at[di, 1 - di], other).wait_recv()
            remote(blk, blk, ap_s.at[n], ap_r.at[n], other).start()

    def share_far():
        far = a_all.at[step(x, 2, 4), c]
        for di in range(2):
            part = a_all.at[step(x, 2, 4), c, pl.ds(96 * di, 96)]
            remote(part, part, af_s.at[di], af_r.at[di], other).wait_recv()
        remote(far, far, ap_s.at[3], ap_r.at[3], other).start()

    def other_core(n, dx):
        blk = a_all.at[step(x, dx, 4), 1 - c]
        remote(blk, blk, ap_s.at[n], ap_r.at[n], other).wait_recv()

    targets = (4, 3, -3, 2, -2, 1, -1, 0)

    def select(q, first, last):
        for j in range(first, last):
            t = step(z, targets[j], 8)
            o = xor3(t, kappa)
            lo, hi = jnp.minimum(t, o), jnp.maximum(t, o)
            kind = jnp.where(kappa == 0, 2, jnp.where(t == lo, 0, 1))
            rows = pl.ds(j * OWN[q], OWN[q])
            for i, (dst, w) in enumerate(((v_one[q], lo), (v_two[q], hi))):
                dst[rows, :] = jnp.dot(
                    sel[q][kind, i], v_buf[q][w].reshape(4 * BLOCK[q], -1), preferred_element_type=jnp.float32
                ).astype(jnp.bfloat16)

    nt = (((1,), (1,)), ((), ()))

    def products(q, g, first, last):
        rows = pl.ds(first * OWN[q], (last - first) * OWN[q])
        rows_a = a_all[step(x, ring[g], 4)].reshape(2 * a_all.shape[2], -1)
        cs[q][g, rows] = lax.dot_general(
            v_one[q][rows, :], rows_a, nt, preferred_element_type=jnp.float32
        ) - lax.dot_general(v_two[q][rows, :], rows_a, nt, preferred_element_type=jnp.float32)

    def part_of(q, t, g):
        j = targets.index(4 if t == -4 else t)
        return cs[q][g, pl.ds(j * OWN[q], OWN[q]), :]

    def streams(g):
        return ((1, 0, 3 + g % 2), (-1, 1, 4 - g % 2))

    def hop(q, g, i, s, d):
        to = dev(x, y, c, step(z, d, 8))
        return (
            remote(sq[q].at[g, i, s], rq[q].at[g, i, s], rq_s.at[q, g, i, s], rq_r.at[q, g, i, s], to),
            remote(ss.at[q, g, i, s], rs.at[q, g, i, s], rs_s.at[q, g, i, s], rs_r.at[q, g, i, s], to),
        )

    def incoming(q, g, i, s, d):
        for cp in hop(q, g, i, s, d):
            cp.wait_recv()
        return dequantize(rq[q][g, i, s], rs[q, g, i, s])

    def advance(q, s, *groups):
        for g in groups:
            for d, i, length in streams(g):
                if s < length:
                    val = part_of(q, d * (length - s), g)
                    if s:
                        val = val + incoming(q, g, i, s - 1, d)
                    quantize(val, sq[q].at[g, i, s], ss.at[q, g, i, s])
                    for cp in hop(q, g, i, s, d):
                        cp.start()

    o_mine = xor3(z, kappa)
    end = jnp.where(z > o_mine, 1, 0)

    def deliver(q, g, dc, mirror):
        xx, cc = step(x, ring[g], 4), step(c, dc, 2)
        lanes = pl.ds(pl.multiple_of(128 * cc, 128), 256)
        slot = 2 * (z if mirror else o_mine) + end
        n, m = g * 2 + dc, int(mirror)
        to = dev(xx, y, cc, o_mine if mirror else z)
        if not (g or dc or mirror):
            return (
                pltpu.make_async_copy(fq[q].at[g, :, lanes], gq[q].at[slot], own_s.at[1, q]),
                pltpu.make_async_copy(fs.at[q, g], gs.at[q, slot], own_s.at[2, q]),
            )
        return (
            remote(fq[q].at[g, :, lanes], gq[q].at[slot], fq_s.at[q, m, n], fq_r.at[q, m, kappa], to),
            remote(fs.at[q, g], gs.at[q, slot], fs_s.at[q, m, n], fs_r.at[q, m, kappa], to),
        )

    def finish(q, *groups):
        for g in groups:
            val = part_of(q, 0, g)
            for d, i, length in streams(g):
                val = val + incoming(q, g, i, length - 1, d)
            quantize(val, fq[q].at[g], fs.at[q, g])

            @pl.when(kappa > 0)
            def _():
                for dc in (0, 1):
                    for cp in deliver(q, g, dc, True):
                        cp.start()

            for dc in (0, 1):
                for cp in deliver(q, g, dc, False):
                    cp.start()

    def arrived(q, m, k):
        remote(fq[q].at[0, :, pl.ds(0, 256)], gq[q].at[0], fq_s.at[q, 0, 0], fq_r.at[q, m, k], other).wait_recv()
        remote(fs.at[q, 0], gs.at[q, 0], fs_s.at[q, 0, 0], fs_r.at[q, m, k], other).wait_recv()

    tn = (((0,), (0,)), ((), ()))

    def assemble(q):
        for dx in (0, 3, 1, 2):
            for dc in range(2):
                k = kid(step(x, dx, 4), step(c, dc, 2))
                if dx or dc:
                    arrived(q, 0, k)
                else:
                    for cp in deliver(q, 0, 0, False):
                        cp.wait()

                @pl.when(k > 0)
                def _():
                    arrived(q, 1, k)

        full = jnp.concatenate([dequantize(gq[q][i], gs[q, i]) for i in range(16)], axis=0)
        top = full.astype(jnp.bfloat16)
        low = (full - top.astype(jnp.float32)).astype(jnp.bfloat16)
        w_rows = w_ref[pl.ds(16 * OWN[0] * q, 16 * OWN[q]), :]
        return lax.dot_general(top, w_rows, tn, preferred_element_type=jnp.float32) + lax.dot_general(
            low, w_rows, tn, preferred_element_type=jnp.float32
        )

    spread(0)
    for cp in inputs[3:]:
        cp.wait()
    table = table_ref[z]
    sign = table[3:4].astype(jnp.float32)

    @pl.loop(0, 9)
    def _(i):
        rows = lax.broadcasted_iota(jnp.int32, (128, 8 * G * G), 0) + i * 128
        hit = rows == table[0:1]
        w_ref[pl.ds(pl.multiple_of(i * 128, 128), 128), :] = jnp.where(hit, sign, 0.0).astype(jnp.bfloat16)

    vir, occ = column(vir_ref[...]), column(occ_ref[...])
    ev_ref[...] = looked_up(table[1:2], vir) + looked_up(table[2:3], vir)
    ep_ref[...] = column(looked_up(pairs_ref[0:1], occ) + looked_up(pairs_ref[1:2], occ))
    for q in range(2):
        gq[q][2 * z + 1] = jnp.zeros(gq[q].shape[1:], gq[q].dtype)
        gs[q, 2 * z + 1] = jnp.zeros(gs.shape[2:], gs.dtype)

    pass_on(0)
    spread(1)
    pass_on_a()
    other_core(0, 0)
    gathered(0)
    select(0, 0, 3)
    products(0, 0, 0, 3)
    advance(0, 0, 0)
    share_near()
    select(0, 3, 8)
    products(0, 0, 3, 8)
    pass_on(1)
    advance(0, 1, 0)
    other_core(2, 1)
    products(0, 1, 0, 8)
    advance(0, 0, 1)
    other_core(1, -1)
    products(0, 2, 0, 8)
    advance(0, 0, 2)
    advance(0, 2, 0)
    share_far()
    advance(0, 1, 1, 2)
    advance(0, 3, 0)
    other_core(3, 2)
    products(0, 3, 0, 8)
    advance(0, 0, 3)
    finish(0, 0)
    advance(0, 2, 1, 2)
    gathered(1)
    select(1, 0, 8)
    products(1, 0, 0, 8)
    products(1, 1, 0, 8)
    advance(1, 0, 0, 1)
    advance(0, 1, 3)
    advance(0, 3, 1, 2)
    products(1, 2, 0, 8)
    products(1, 3, 0, 8)
    advance(1, 0, 2, 3)
    finish(0, 1, 2)
    advance(0, 2, 3)
    advance(1, 1, 0, 1, 2, 3)
    advance(0, 3, 3)
    advance(1, 2, 0, 1, 2, 3)
    finish(0, 3)
    advance(1, 3, 0, 1, 2, 3)
    finish(1, 0, 1, 2, 3)
    o_ref[...] = assemble(0)
    o_ref[...] = o_ref[...] + assemble(1)
    leaving = []
    for i in range(3):
        rows = pl.ds(64 * i, 64)
        out_ref[rows, :] = o_ref[pl.ds(pl.multiple_of(64 * (c + i), 8), 64), :] / (ep_ref[rows, :] - ev_ref[...])
        leaving.append(pltpu.make_async_copy(out_ref.at[rows], out_hbm.at[rows], out_s.at[i]))
        leaving[-1].start()

    for q in range(2):
        for n in range(8):
            blk = v_buf[q].at[0, 0]
            if n:
                remote(blk, blk, vx_s.at[q, n], vx_r.at[q, 0], other).wait_send()
            for di in range(2):
                remote(blk, blk, vy_s.at[q, di, n], vx_r.at[q, 0], other).wait_send()
            remote(blk, blk, vf_s.at[q, n], vx_r.at[q, 0], other).wait_send()
    half_a = a_all.at[0, 0, pl.ds(0, 96)]
    for di in range(2):
        for h in range(2):
            remote(half_a, half_a, ax_s.at[di, h], ax_r.at[di, h], other).wait_send()
        remote(half_a, half_a, af_s.at[di], af_r.at[di], other).wait_send()
    for n in range(4):
        remote(a_ref, a_ref, ap_s.at[n], ap_r.at[n], other).wait_send()
    for q in range(2):
        for g in range(4):
            for d, i, length in streams(g):
                for s in range(length):
                    for cp in hop(q, g, i, s, d):
                        cp.wait_send()
            for dc in (0, 1):
                if g or dc:
                    for cp in deliver(q, g, dc, False):
                        cp.wait_send()

    @pl.when(kappa > 0)
    def _():
        for q in range(2):
            for g in range(4):
                for dc in (0, 1):
                    for cp in deliver(q, g, dc, True):
                        cp.wait_send()

    for cp in leaving:
        cp.wait()


def on_device(amplitudes, integrals, pair_index, eps_occ, eps_vir):
    rows, depth = amplitudes.shape
    f32, bf16, i16 = jnp.float32, jnp.bfloat16, jnp.int16
    dma = pltpu.SemaphoreType.DMA
    sel0, sel1 = [jnp.asarray(s, bf16) for s in selection_tables()]
    order, table = jnp.asarray(row_order(), bf16), jnp.asarray(output_tables())
    vt, pairs, occ, vir = integrals.T, pair_index.T, eps_occ.reshape(1, -1), eps_vir.reshape(1, -1)

    def both(shape, dtype):
        return [pltpu.VMEM(shape(BLOCK[q], OWN[q]), dtype) for q in range(2)]

    return pl.pallas_call(
        kernel,
        out_shape=jax.ShapeDtypeStruct((rows, 8 * G * G), f32),
        in_specs=[pl.BlockSpec(memory_space=pl.ANY)] * 9,
        out_specs=pl.BlockSpec(memory_space=pl.ANY),
        scratch_shapes=[
            *[pltpu.VMEM(a.shape, a.dtype) for a in (sel0, sel1, order, table, vt, pairs, occ, vir)],
            dma((9,)),
            dma((3,)),
            pltpu.VMEM((rows, 8 * G * G), f32),
            pltpu.VMEM((4, 2, rows, depth), bf16),
            pltpu.VMEM((8 * G * G, 8 * G * G), bf16),
            pltpu.VMEM((256, 8 * G * G), f32),
            pltpu.VMEM((rows, 1), f32),
            pltpu.VMEM((1, 8 * G * G), f32),
            *both(lambda b, n: (8, b, depth), bf16),
            *both(lambda b, n: (8, 4, b, depth), bf16),
            *both(lambda b, n: (8 * n, depth), bf16),
            *both(lambda b, n: (8 * n, depth), bf16),
            *both(lambda b, n: (4, 8 * n, 2 * rows), f32),
            *both(lambda b, n: (4, 2, 4, n, 2 * rows), i16),
            *both(lambda b, n: (4, 2, 4, n, 2 * rows), i16),
            *both(lambda b, n: (4, n, 2 * rows), i16),
            *both(lambda b, n: (16, n, 256), i16),
            pltpu.VMEM((2, 4, 2, 4, 8, 128), bf16),
            pltpu.VMEM((2, 4, 2, 4, 8, 128), bf16),
            pltpu.VMEM((2, 4, 8, 128), bf16),
            pltpu.VMEM((2, 16, 8, 128), bf16),
            dma((2, 8)), dma((2, 8)), dma((2, 2, 8)), dma((2, 2, 8)), dma((2, 8)), dma((2, 8)),
            dma((2, 2)), dma((2, 2)), dma((2,)), dma((2,)), dma((4,)), dma((4,)), dma((3, 2)),
            dma((2, 4, 2, 4)), dma((2, 4, 2, 4)), dma((2, 4, 2, 4)), dma((2, 4, 2, 4)),
            dma((2, 2, 8)), dma((2, 2, 8)), dma((2, 2, 8)), dma((2, 2, 8)),
        ],
        compiler_params=pltpu.CompilerParams(
            collective_id=0, has_side_effects=True, vmem_limit_bytes=60 * 1024 * 1024
        ),
    )(sel0, sel1, order, table, amplitudes, vt, pairs, occ, vir)


def solution(mesh):
    in_specs = (P("pair", "slab"), P("slab", "pair"), P("pair", None), P(), P())
    return jax.shard_map(on_device, mesh=mesh, in_specs=in_specs, out_specs=P("pair", "slab"), check_vma=False)
```

```python
import functools

import jax
import jax.numpy as jnp
import numpy as np
from jax import lax
from jax.experimental import pallas as pl
from jax.experimental.pallas import tpu as pltpu
from jax.sharding import PartitionSpec as P

MESH = pl.DeviceIdType.MESH
G = 12
BLOCK = (16, 24)
OWN = (24, 48)
QMAX = 32767.0


def chunk_of(u, v):
    return 1 if (u + v) % 3 else 0


def block_row(u, v):
    q = chunk_of(u, v)
    rank = sum(chunk_of(u, i) == q for i in range(v))
    return BLOCK[q] * (u // 3) + (4, 8)[q] * (u % 3) + rank


def own_row(i, v):
    q = chunk_of(i, v)
    return (4, 8)[q] * i + sum(chunk_of(i, j) == q for j in range(v))


def selection_tables():
    sel = [np.zeros((3, 2, OWN[q], 4 * BLOCK[q]), np.float32) for q in range(2)]
    for kind in range(3):
        for i in range(6):
            for v in range(G):
                u, vv = i, v
                if kind == 1:
                    u = i + 6
                if kind == 2 and v < i:
                    u, vv = i + 6, v + 6
                q = chunk_of(i, v)
                sel[q][kind, 0, own_row(i, v), block_row(u, vv)] = 1
                sel[q][kind, 1, own_row(i, v), block_row(vv, u)] = 1
    return sel


def output_tables():
    table = np.zeros((8, 4, G * 8 * G), np.int32)
    for w in range(8):
        for a in range(G):
            for o in range(8):
                for b in range(G):
                    col = (a * 8 + o) * G + b
                    if o > w:
                        u, v, s, h = a, b, 1, a // 6
                    elif o < w:
                        u, v, s, h = b, a, -1, b // 6
                    else:
                        lo, hi, s, h = min(a, b), max(a, b), (0 if a == b else 1 if a < b else -1), 0
                        if lo >= 6:
                            u, v, s = hi - 6, lo - 6, -s
                        else:
                            u, v = lo, hi
                    q = chunk_of(u, v)
                    row = 16 * OWN[0] * q + (o * 2 + h) * OWN[q] + own_row(u % 6, v)
                    table[w, :, col] = row, w * G + a, o * G + b, s
    return table


def row_order():
    order = np.zeros((8 * sum(BLOCK), 3 * 8 * G), np.float32)
    for o in range(8):
        for a in range(3):
            for b in range(G):
                q = chunk_of(a, b)
                order[8 * BLOCK[0] * q + o * BLOCK[q] + block_row(a, b), (a * 8 + o) * G + b] = 1
    return order


def xor3(a, b):
    out = 0
    for bit in (1, 2, 4):
        out = out + bit * lax.rem(lax.div(a, bit) + lax.div(b, bit), 2)
    return out


def quantize(val, q_ref, s_ref):
    r, width = val.shape
    cube = val.reshape(r // 8, 8, width)
    top = jnp.max(jnp.abs(cube), axis=0)
    top = functools.reduce(jnp.maximum, [top[:, 128 * i : 128 * (i + 1)] for i in range(width // 128)])
    top = jnp.maximum(top * (1.01 / QMAX), 1e-36).astype(jnp.bfloat16)
    inv = 1.0 / top.astype(jnp.float32)
    q = (cube * jnp.concatenate([inv] * (width // 128), axis=1) + 32768.5).astype(jnp.int32) - 32768
    q_ref[...] = q.reshape(r, width).astype(jnp.int16)
    s_ref[...] = top


def dequantize(q, s):
    r, width = q.shape
    cube = q.astype(jnp.int32).astype(jnp.float32).reshape(r // 8, 8, width)
    return (cube * jnp.concatenate([s.astype(jnp.float32)] * (width // 128), axis=1)).reshape(r, width)


def column(row):
    n = row.shape[1]
    same = lax.broadcasted_iota(jnp.int32, (n, n), 0) == lax.broadcasted_iota(jnp.int32, (n, n), 1)
    return jnp.sum(jnp.where(same, row, 0.0), axis=1, keepdims=True)


def looked_up(ids, table):
    hit = lax.broadcasted_iota(jnp.int32, (table.shape[0], ids.shape[1]), 0) == ids
    return jnp.sum(jnp.where(hit, table, 0.0), axis=0, keepdims=True)


def kernel(sel0_hbm, sel1_hbm, order_hbm, table_hbm, a_hbm, vt_hbm, pairs_hbm, occ_hbm, vir_hbm, out_hbm,
           sel0, sel1, order_ref, table_ref, vt_ref, pairs_ref, occ_ref, vir_ref, in_s, out_s, out_ref,
           a_all, w_ref, o_ref, ep_ref, ev_ref,
           vl0, vl1, vb0, vb1, va0, va1, vc0, vc1, cs0, cs1, rq0, rq1, sq0, sq1, fq0, fq1, gq0, gq1,
           rs, ss, fs, gs,
           vx_s, vx_r, vy_s, vy_r, vf_s, vf_r, ax_s, ax_r, af_s, af_r, ap_s, ap_r, own_s,
           rq_s, rq_r, rs_s, rs_r, fq_s, fq_r, fs_s, fs_r):
    sel, v_local, v_buf, v_one, v_two, cs = (sel0, sel1), (vl0, vl1), (vb0, vb1), (va0, va1), (vc0, vc1), (cs0, cs1)
    rq, sq, fq, gq = (rq0, rq1), (sq0, sq1), (fq0, fq1), (gq0, gq1)
    pair, z = lax.axis_index("pair"), lax.axis_index("slab")
    x, y, c = lax.div(pair, 8), lax.rem(lax.div(pair, 2), 4), lax.rem(pair, 2)

    def kid(xx, cc):
        return xx + 4 * cc

    kappa = kid(x, c)
    w_mine = lax.div(pair, 4)

    def dev(xx, yy, cc, zz):
        return ((xx * 4 + yy) * 2 + cc, zz)

    def step(i, d, n):
        return lax.rem(i + d + n, n)

    def remote(src, dst, ssem, rsem, to):
        return pltpu.make_async_remote_copy(
            src_ref=src, dst_ref=dst, send_sem=ssem, recv_sem=rsem, device_id=to, device_id_type=MESH
        )

    other = dev(x, y, 1 - c, z)
    a_ref = a_all.at[x, c]
    inputs = [
        pltpu.make_async_copy(src, dst, in_s.at[i])
        for i, (src, dst) in enumerate(
            (
                (order_hbm, order_ref), (vt_hbm, vt_ref), (a_hbm, a_ref), (table_hbm, table_ref), (sel0_hbm, sel0),
                (sel1_hbm, sel1), (pairs_hbm, pairs_ref), (occ_hbm, occ_ref), (vir_hbm, vir_ref),
            )
        )
    ]
    for cp in inputs:
        cp.start()

    barrier = pltpu.get_barrier_semaphore()

    def greet(to):
        pl.semaphore_signal(barrier, inc=1, device_id=to, device_id_type=MESH)

    for dx in range(4):
        for dc in range(2):
            if dx or dc:
                greet(dev(step(x, dx, 4), y, step(c, dc, 2), z))
    for d in (1, -1):
        greet(dev(x, step(y, d, 4), c, z))
        greet(dev(x, y, c, step(z, d, 8)))
    inputs[0].wait()
    inputs[1].wait()
    ordered = jnp.dot(order_ref[...], vt_ref[...], preferred_element_type=jnp.float32).astype(jnp.bfloat16)
    v_local[0][...] = ordered[: 8 * BLOCK[0]].reshape(v_local[0].shape)
    v_local[1][...] = ordered[8 * BLOCK[0] :].reshape(v_local[1].shape)
    pl.semaphore_wait(barrier, 11)

    slot_y = lax.rem(y, 2) * 2
    ring = (0, 1, 3, 2)

    def to_class(q, dx, dc):
        xx, cc = step(x, dx, 4), step(c, dc, 2)
        src = v_local[q].at[xor3(w_mine, kid(xx, cc))]
        dst = v_buf[q].at[w_mine, slot_y + c]
        if dx or dc:
            return remote(src, dst, vx_s.at[q, dx * 2 + dc], vx_r.at[q, kappa], dev(xx, y, cc, z))
        return pltpu.make_async_copy(src, dst, own_s.at[0, q])

    for q in range(2):
        for dx in (1, 3, 2, 0):
            for dc in (0, 1):
                to_class(q, dx, dc).start()
    inputs[2].wait()
    for h in range(2):
        for d, di in ((1, 0), (-1, 1)):
            hh = h if di == 0 else 1 - h
            part = a_all.at[x, c, pl.ds(96 * hh, 96)]
            remote(part, part, ax_s.at[di, hh], ax_r.at[di, hh], dev(step(x, d, 4), y, c, z)).start()
    remote(a_ref, a_ref, ap_s.at[0], ap_r.at[0], other).start()

    def v_slot(q, yy, xx, cc):
        return v_buf[q].at[2 * xx + lax.div(yy, 2), lax.rem(yy, 2) * 2 + cc]

    def to_y(d):
        return dev(x, step(y, d, 4), c, z)

    def spread(q):
        for dx in ring:
            for dc in range(2):
                xx, cc = step(x, dx, 4), step(c, dc, 2)
                blk = v_slot(q, y, xx, cc)
                if dx or dc:
                    remote(blk, blk, vx_s.at[q, 0], vx_r.at[q, kid(xx, cc)], other).wait_recv()
                else:
                    to_class(q, 0, 0).wait()
                for d, di in ((1, 0), (-1, 1)):
                    u = dx * 2 + cc
                    remote(blk, blk, vy_s.at[q, di, u], vy_r.at[q, di, u], to_y(d)).start()

    def pass_on(q):
        for dx in ring:
            for d, di in ((1, 0), (-1, 1)):
                u = dx * 2 + di
                blk = v_slot(q, step(y, -d, 4), step(x, dx, 4), di)
                remote(blk, blk, vy_s.at[q, di, u], vy_r.at[q, di, u], other).wait_recv()
                remote(blk, blk, vf_s.at[q, u], vf_r.at[q, u], to_y(d)).start()

    def gathered(q):
        for d, di in ((1, 0), (-1, 1)):
            for dx in ring:
                u = dx * 2 + 1 - di
                blk = v_slot(q, step(y, -d, 4), step(x, dx, 4), 1 - di)
                remote(blk, blk, vy_s.at[q, di, u], vy_r.at[q, di, u], other).wait_recv()
        for dx in ring:
            for di in range(2):
                u = dx * 2 + di
                blk = v_slot(q, step(y, 2, 4), step(x, dx, 4), di)
                remote(blk, blk, vf_s.at[q, u], vf_r.at[q, u], other).wait_recv()

    def pass_on_a():
        for d, di in ((1, 0), (-1, 1)):
            blk = a_all.at[step(x, -d, 4), c, pl.ds(96 * di, 96)]
            remote(blk, blk, ax_s.at[di, di], ax_r.at[di, di], other).wait_recv()
            remote(blk, blk, af_s.at[di], af_r.at[di], dev(step(x, d, 4), y, c, z)).start()

    def share_near():
        for n, d, di in ((1, 1, 0), (2, -1, 1)):
            blk = a_all.at[step(x, -d, 4), c]
            part = a_all.at[step(x, -d, 4), c, pl.ds(96 * (1 - di), 96)]
            remote(part, part, ax_s.at[di, 1 - di], ax_r.at[di, 1 - di], other).wait_recv()
            remote(blk, blk, ap_s.at[n], ap_r.at[n], other).start()

    def share_far():
        far = a_all.at[step(x, 2, 4), c]
        for di in range(2):
            part = a_all.at[step(x, 2, 4), c, pl.ds(96 * di, 96)]
            remote(part, part, af_s.at[di], af_r.at[di], other).wait_recv()
        remote(far, far, ap_s.at[3], ap_r.at[3], other).start()

    def other_core(n, dx):
        blk = a_all.at[step(x, dx, 4), 1 - c]
        remote(blk, blk, ap_s.at[n], ap_r.at[n], other).wait_recv()

    targets = (4, 3, -3, 2, -2, 1, -1, 0)

    def select(q, first, last):
        for j in range(first, last):
            t = step(z, targets[j], 8)
            o = xor3(t, kappa)
            lo, hi = jnp.minimum(t, o), jnp.maximum(t, o)
            kind = jnp.where(kappa == 0, 2, jnp.where(t == lo, 0, 1))
            rows = pl.ds(j * OWN[q], OWN[q])
            for i, (dst, w) in enumerate(((v_one[q], lo), (v_two[q], hi))):
                dst[rows, :] = jnp.dot(
                    sel[q][kind, i], v_buf[q][w].reshape(4 * BLOCK[q], -1), preferred_element_type=jnp.float32
                ).astype(jnp.bfloat16)

    nt = (((1,), (1,)), ((), ()))

    def products(q, g, first, last):
        rows = pl.ds(first * OWN[q], (last - first) * OWN[q])
        rows_a = a_all[step(x, ring[g], 4)].reshape(2 * a_all.shape[2], -1)
        cs[q][g, rows] = lax.dot_general(
            v_one[q][rows, :], rows_a, nt, preferred_element_type=jnp.float32
        ) - lax.dot_general(v_two[q][rows, :], rows_a, nt, preferred_element_type=jnp.float32)

    def part_of(q, t, g):
        j = targets.index(4 if t == -4 else t)
        return cs[q][g, pl.ds(j * OWN[q], OWN[q]), :]

    def streams(g):
        return ((1, 0, 3 + g % 2), (-1, 1, 4 - g % 2))

    def hop(q, g, i, s, d):
        to = dev(x, y, c, step(z, d, 8))
        return (
            remote(sq[q].at[g, i, s], rq[q].at[g, i, s], rq_s.at[q, g, i, s], rq_r.at[q, g, i, s], to),
            remote(ss.at[q, g, i, s], rs.at[q, g, i, s], rs_s.at[q, g, i, s], rs_r.at[q, g, i, s], to),
        )

    def incoming(q, g, i, s, d):
        for cp in hop(q, g, i, s, d):
            cp.wait_recv()
        return dequantize(rq[q][g, i, s], rs[q, g, i, s])

    def advance(q, s, *groups):
        for g in groups:
            for d, i, length in streams(g):
                if s < length:
                    val = part_of(q, d * (length - s), g)
                    if s:
                        val = val + incoming(q, g, i, s - 1, d)
                    quantize(val, sq[q].at[g, i, s], ss.at[q, g, i, s])
                    for cp in hop(q, g, i, s, d):
                        cp.start()

    o_mine = xor3(z, kappa)
    end = jnp.where(z > o_mine, 1, 0)

    def deliver(q, g, dc, mirror):
        xx, cc = step(x, ring[g], 4), step(c, dc, 2)
        lanes = pl.ds(pl.multiple_of(128 * cc, 128), 256)
        slot = 2 * (z if mirror else o_mine) + end
        n, m = g * 2 + dc, int(mirror)
        to = dev(xx, y, cc, o_mine if mirror else z)
        if not (g or dc or mirror):
            return (
                pltpu.make_async_copy(fq[q].at[g, :, lanes], gq[q].at[slot], own_s.at[1, q]),
                pltpu.make_async_copy(fs.at[q, g], gs.at[q, slot], own_s.at[2, q]),
            )
        return (
            remote(fq[q].at[g, :, lanes], gq[q].at[slot], fq_s.at[q, m, n], fq_r.at[q, m, kappa], to),
            remote(fs.at[q, g], gs.at[q, slot], fs_s.at[q, m, n], fs_r.at[q, m, kappa], to),
        )

    def finish(q, *groups):
        for g in groups:
            val = part_of(q, 0, g)
            for d, i, length in streams(g):
                val = val + incoming(q, g, i, length - 1, d)
            quantize(val, fq[q].at[g], fs.at[q, g])

            @pl.when(kappa > 0)
            def _():
                for dc in (0, 1):
                    for cp in deliver(q, g, dc, True):
                        cp.start()

            for dc in (0, 1):
                for cp in deliver(q, g, dc, False):
                    cp.start()

    def arrived(q, m, k):
        remote(fq[q].at[0, :, pl.ds(0, 256)], gq[q].at[0], fq_s.at[q, 0, 0], fq_r.at[q, m, k], other).wait_recv()
        remote(fs.at[q, 0], gs.at[q, 0], fs_s.at[q, 0, 0], fs_r.at[q, m, k], other).wait_recv()

    tn = (((0,), (0,)), ((), ()))

    def assemble(q):
        for dx in (0, 3, 1, 2):
            for dc in range(2):
                k = kid(step(x, dx, 4), step(c, dc, 2))
                if dx or dc:
                    arrived(q, 0, k)
                else:
                    for cp in deliver(q, 0, 0, False):
                        cp.wait()

                @pl.when(k > 0)
                def _():
                    arrived(q, 1, k)

        full = jnp.concatenate([dequantize(gq[q][i], gs[q, i]) for i in range(16)], axis=0)
        top = full.astype(jnp.bfloat16)
        low = (full - top.astype(jnp.float32)).astype(jnp.bfloat16)
        w_rows = w_ref[pl.ds(16 * OWN[0] * q, 16 * OWN[q]), :]
        return lax.dot_general(top, w_rows, tn, preferred_element_type=jnp.float32) + lax.dot_general(
            low, w_rows, tn, preferred_element_type=jnp.float32
        )

    spread(0)
    pass_on(0)
    spread(1)
    for cp in inputs[3:]:
        cp.wait()
    table = table_ref[z]
    sign = table[3:4].astype(jnp.float32)

    @pl.loop(0, 9)
    def _(i):
        rows = lax.broadcasted_iota(jnp.int32, (128, 8 * G * G), 0) + i * 128
        hit = rows == table[0:1]
        w_ref[pl.ds(pl.multiple_of(i * 128, 128), 128), :] = jnp.where(hit, sign, 0.0).astype(jnp.bfloat16)

    vir, occ = column(vir_ref[...]), column(occ_ref[...])
    ev_ref[...] = looked_up(table[1:2], vir) + looked_up(table[2:3], vir)
    ep_ref[...] = column(looked_up(pairs_ref[0:1], occ) + looked_up(pairs_ref[1:2], occ))
    for q in range(2):
        gq[q][2 * z + 1] = jnp.zeros(gq[q].shape[1:], gq[q].dtype)
        gs[q, 2 * z + 1] = jnp.zeros(gs.shape[2:], gs.dtype)

    pass_on_a()
    other_core(0, 0)
    gathered(0)
    select(0, 0, 8)
    products(0, 0, 0, 8)
    advance(0, 0, 0)
    share_near()
    pass_on(1)
    other_core(2, 1)
    products(0, 1, 0, 8)
    advance(0, 0, 1)
    other_core(1, -1)
    products(0, 2, 0, 8)
    advance(0, 0, 2)
    advance(0, 1, 0)
    share_far()
    advance(0, 1, 1, 2)
    advance(0, 2, 0)
    other_core(3, 2)
    products(0, 3, 0, 8)
    advance(0, 0, 3)
    advance(0, 2, 1, 2)
    advance(0, 3, 0)
    gathered(1)
    select(1, 0, 3)
    products(1, 0, 0, 3)
    advance(1, 0, 0)
    products(1, 1, 0, 3)
    advance(1, 0, 1)
    advance(0, 1, 3)
    advance(0, 3, 1, 2)
    products(1, 2, 0, 3)
    advance(1, 0, 2)
    products(1, 3, 0, 3)
    advance(1, 0, 3)
    select(1, 3, 8)
    products(1, 0, 3, 8)
    products(1, 1, 3, 8)
    advance(1, 1, 0, 1)
    advance(0, 2, 3)
    products(1, 2, 3, 8)
    products(1, 3, 3, 8)
    advance(1, 1, 2, 3)
    finish(0, 0, 1, 2)
    advance(1, 2, 0, 1)
    advance(0, 3, 3)
    advance(1, 2, 2, 3)
    advance(1, 3, 0, 1)
    finish(0, 3)
    advance(1, 3, 2, 3)
    finish(1, 3, 1, 2, 0)
    o_ref[...] = assemble(0)
    o_ref[...] = o_ref[...] + assemble(1)
    leaving = []
    for i in range(3):
        rows = pl.ds(64 * i, 64)
        out_ref[rows, :] = o_ref[pl.ds(pl.multiple_of(64 * (c + i), 8), 64), :] / (ep_ref[rows, :] - ev_ref[...])
        leaving.append(pltpu.make_async_copy(out_ref.at[rows], out_hbm.at[rows], out_s.at[i]))
        leaving[-1].start()

    for q in range(2):
        for n in range(8):
            blk = v_buf[q].at[0, 0]
            if n:
                remote(blk, blk, vx_s.at[q, n], vx_r.at[q, 0], other).wait_send()
            for di in range(2):
                remote(blk, blk, vy_s.at[q, di, n], vx_r.at[q, 0], other).wait_send()
            remote(blk, blk, vf_s.at[q, n], vx_r.at[q, 0], other).wait_send()
    half_a = a_all.at[0, 0, pl.ds(0, 96)]
    for di in range(2):
        for h in range(2):
            remote(half_a, half_a, ax_s.at[di, h], ax_r.at[di, h], other).wait_send()
        remote(half_a, half_a, af_s.at[di], af_r.at[di], other).wait_send()
    for n in range(4):
        remote(a_ref, a_ref, ap_s.at[n], ap_r.at[n], other).wait_send()
    for q in range(2):
        for g in range(4):
            for d, i, length in streams(g):
                for s in range(length):
                    for cp in hop(q, g, i, s, d):
                        cp.wait_send()
            for dc in (0, 1):
                if g or dc:
                    for cp in deliver(q, g, dc, False):
                        cp.wait_send()

    @pl.when(kappa > 0)
    def _():
        for q in range(2):
            for g in range(4):
                for dc in (0, 1):
                    for cp in deliver(q, g, dc, True):
                        cp.wait_send()

    for cp in leaving:
        cp.wait()


def on_device(amplitudes, integrals, pair_index, eps_occ, eps_vir):
    rows, depth = amplitudes.shape
    f32, bf16, i16 = jnp.float32, jnp.bfloat16, jnp.int16
    dma = pltpu.SemaphoreType.DMA
    sel0, sel1 = [jnp.asarray(s, bf16) for s in selection_tables()]
    order, table = jnp.asarray(row_order(), bf16), jnp.asarray(output_tables())
    vt, pairs, occ, vir = integrals.T, pair_index.T, eps_occ.reshape(1, -1), eps_vir.reshape(1, -1)

    def both(shape, dtype):
        return [pltpu.VMEM(shape(BLOCK[q], OWN[q]), dtype) for q in range(2)]

    return pl.pallas_call(
        kernel,
        out_shape=jax.ShapeDtypeStruct((rows, 8 * G * G), f32),
        in_specs=[pl.BlockSpec(memory_space=pl.ANY)] * 9,
        out_specs=pl.BlockSpec(memory_space=pl.ANY),
        scratch_shapes=[
            *[pltpu.VMEM(a.shape, a.dtype) for a in (sel0, sel1, order, table, vt, pairs, occ, vir)],
            dma((9,)),
            dma((3,)),
            pltpu.VMEM((rows, 8 * G * G), f32),
            pltpu.VMEM((4, 2, rows, depth), bf16),
            pltpu.VMEM((8 * G * G, 8 * G * G), bf16),
            pltpu.VMEM((256, 8 * G * G), f32),
            pltpu.VMEM((rows, 1), f32),
            pltpu.VMEM((1, 8 * G * G), f32),
            *both(lambda b, n: (8, b, depth), bf16),
            *both(lambda b, n: (8, 4, b, depth), bf16),
            *both(lambda b, n: (8 * n, depth), bf16),
            *both(lambda b, n: (8 * n, depth), bf16),
            *both(lambda b, n: (4, 8 * n, 2 * rows), f32),
            *both(lambda b, n: (4, 2, 4, n, 2 * rows), i16),
            *both(lambda b, n: (4, 2, 4, n, 2 * rows), i16),
            *both(lambda b, n: (4, n, 2 * rows), i16),
            *both(lambda b, n: (16, n, 256), i16),
            pltpu.VMEM((2, 4, 2, 4, 8, 128), bf16),
            pltpu.VMEM((2, 4, 2, 4, 8, 128), bf16),
            pltpu.VMEM((2, 4, 8, 128), bf16),
            pltpu.VMEM((2, 16, 8, 128), bf16),
            dma((2, 8)), dma((2, 8)), dma((2, 2, 8)), dma((2, 2, 8)), dma((2, 8)), dma((2, 8)),
            dma((2, 2)), dma((2, 2)), dma((2,)), dma((2,)), dma((4,)), dma((4,)), dma((3, 2)),
            dma((2, 4, 2, 4)), dma((2, 4, 2, 4)), dma((2, 4, 2, 4)), dma((2, 4, 2, 4)),
            dma((2, 2, 8)), dma((2, 2, 8)), dma((2, 2, 8)), dma((2, 2, 8)),
        ],
        compiler_params=pltpu.CompilerParams(
            collective_id=0, has_side_effects=True, vmem_limit_bytes=60 * 1024 * 1024
        ),
    )(sel0, sel1, order, table, amplitudes, vt, pairs, occ, vir)


def solution(mesh):
    in_specs = (P("pair", "slab"), P("slab", "pair"), P("pair", None), P(), P())
    return jax.shard_map(on_device, mesh=mesh, in_specs=in_specs, out_specs=P("pair", "slab"), check_vma=False)
```
